512 devices in a mesh: section: 16 (over z_lo, core), seq: 32 (over y, x, z_hi).
Axes of the slice: x: 4, y: 4, z: 16 (z_hi: 2, z_lo: 8; z = z_hi * 8 + z_lo), core: 2. Of those that a mesh axis runs over, the one named last changes fastest.
Arguments:
- query_row: bfloat16 [16, 8192, 512], P('section', 'seq'), may hold values from -80 to 80
- key_row: bfloat16 [16, 8192, 512], P('section', 'seq'), may hold values from -4 to 4
- value_row: bfloat16 [16, 8192, 512], P('section', 'seq'), may hold values from -6 to 6
- cotangent_row: bfloat16 [16, 8192, 512], P('section', 'seq'), may hold values from -6 to 6
- query_col: bfloat16 [16, 8192, 512], P('section', 'seq'), may hold values from -80 to 80
- key_col: bfloat16 [16, 8192, 512], P('section', 'seq'), may hold values from -4 to 4
- value_col: bfloat16 [16, 8192, 512], P('section', 'seq'), may hold values from -6 to 6
- cotangent_col: bfloat16 [16, 8192, 512], P('section', 'seq'), may hold values from -6 to 6
Outputs:
- upstream: bfloat16 [16, 8192, 3072], P('section', 'seq')
The draws below stay inside these ranges and needn't reach their ends.
All inputs are finite; a program needn't handle non-finite values.
Results may differ from the reference program's by a relative error of at most 0.013.
Values may be sent and summed in bfloat16 or wider, within the bound.
No kernel may reach another device: no remote copies, remote signals or barrier semaphores. Data moves between devices by JAX's collectives and lax.ppermute only.
A program may use at most 64 MiB of HBM per device.

```python
import jax
import jax.numpy as jnp
from jax import lax

H_ROW = 4
H_COL = 4
HD = 128
COLS = 256
SECTIONS = 16
GRID_ROWS = 32
TOKENS = 8192


def paired(key, salt, heads):
    key = jax.random.fold_in(key, salt)
    shape = (SECTIONS, TOKENS, heads, HD)
    base_keys = jnp.clip(jax.random.normal(jax.random.fold_in(key, 1), shape, jnp.float32), -4.0, 4.0)
    drawn_query = jnp.clip(jax.random.normal(jax.random.fold_in(key, 2), shape, jnp.float32), -4.0, 4.0)
    keys_out = base_keys
    query_out = drawn_query
    return (query_out.reshape(SECTIONS, TOKENS, heads * HD), keys_out.reshape(SECTIONS, TOKENS, heads * HD))


def draw_query_row(key, part):
    return paired(key, 11, H_ROW)[0].astype(jnp.bfloat16)


def draw_key_row(key, part):
    return paired(key, 11, H_ROW)[1].astype(jnp.bfloat16)


def draw_query_col(key, part):
    return paired(key, 12, H_COL)[0].astype(jnp.bfloat16)


def draw_key_col(key, part):
    return paired(key, 12, H_COL)[1].astype(jnp.bfloat16)


def level_of(stream_key, shape, pieces, smallest, high):
    factor_of = 1.0
    for dim, blocks in pieces:
        draws = jax.random.uniform(jax.random.fold_in(jax.random.fold_in(stream_key, 6), dim), (blocks,), jnp.float32, smallest / len(pieces), high / len(pieces))
        factor_of = factor_of * jnp.repeat(jnp.exp(draws), shape[dim] // blocks).reshape((-1,) + (1,) * (len(shape) - 1 - dim))
    return factor_of


def centred(key, extent, width, reach, pieces=(), dtype=jnp.bfloat16):
    gain = level_of(key, extent, pieces, -0.22, 0.18) if pieces else 1.0
    drawn = jax.random.normal(key, extent, jnp.float32) * width * gain
    return jnp.minimum(jnp.maximum(drawn, -reach), reach).astype(dtype)


def setup_inputs(seed: int = 0) -> dict:
    key_list = jax.random.split(jax.random.key(seed), 9)
    query_row = draw_query_row(jax.random.fold_in(key_list[8], 71), 0)
    key_row = draw_key_row(jax.random.fold_in(key_list[8], 71), 0)
    value_row = centred(key_list[2], (SECTIONS, TOKENS, H_ROW * HD), 1.0, 6.0, ((0, 16), (1, 32)))
    cotangent_row = centred(key_list[3], (SECTIONS, TOKENS, H_ROW * HD), 1.0, 6.0, ((0, 16), (1, 32)))
    query_col = draw_query_col(jax.random.fold_in(key_list[8], 71), 0)
    key_col = draw_key_col(jax.random.fold_in(key_list[8], 71), 0)
    value_col = centred(key_list[6], (SECTIONS, TOKENS, H_COL * HD), 1.0, 6.0, ((0, 16), (1, 32)))
    cotangent_col = centred(key_list[7], (SECTIONS, TOKENS, H_COL * HD), 1.0, 6.0, ((0, 16), (1, 32)))
    return {"query_row": query_row, "key_row": key_row, "value_row": value_row, "cotangent_row": cotangent_row, "query_col": query_col, "key_col": key_col, "value_col": value_col, "cotangent_col": cotangent_col}


def attend_back(queries, keys_in, values, grad_out):
    length = queries.shape[1]
    scaling = queries.shape[3] ** -0.5
    query_f = queries.astype(jnp.float32)
    key_f = keys_in.astype(jnp.float32)
    value_f = values.astype(jnp.float32)
    grad_f = grad_out.astype(jnp.float32)
    scores = jnp.einsum("blhe,bmhe->bhlm", query_f, key_f, preferred_element_type=jnp.float32) * scaling
    causal = jnp.arange(length)[:, None] >= jnp.arange(length)[None, :]
    scores = jnp.where(causal, scores, -1e30)
    largest = jnp.max(scores, axis=-1, keepdims=True)
    weights = jnp.exp(scores - largest)
    probability = weights / jnp.sum(weights, axis=-1, keepdims=True)
    prob_low = probability.astype(jnp.bfloat16).astype(jnp.float32)
    attended = jnp.einsum("bhlm,bmhe->blhe", prob_low, value_f, preferred_element_type=jnp.float32)
    inner_sum = jnp.sum(grad_f * attended, axis=-1)
    grad_probs = jnp.einsum("blhe,bmhe->bhlm", grad_f, value_f, preferred_element_type=jnp.float32)
    grad_scores = probability * (grad_probs - jnp.transpose(inner_sum, (0, 2, 1))[..., None]) * scaling
    grad_low = grad_scores.astype(jnp.bfloat16).astype(jnp.float32)
    grad_query = jnp.einsum("bhlm,bmhe->blhe", grad_low, key_f, preferred_element_type=jnp.float32)
    grad_key = jnp.einsum("bhlm,blhe->bmhe", grad_low, query_f, preferred_element_type=jnp.float32)
    grad_value = jnp.einsum("bhlm,blhe->bmhe", prob_low, grad_f, preferred_element_type=jnp.float32)
    return (grad_query.astype(jnp.bfloat16), grad_key.astype(jnp.bfloat16), grad_value.astype(jnp.bfloat16))


def section_grads(arrays):
    query_row, key_row, value_row, cotangent_row, query_col, key_col, value_col, cotangent_col = arrays

    def as_rows(block, heads):
        return block.reshape(GRID_ROWS, COLS, heads, HD)

    def as_cols(block, heads):
        return jnp.transpose(block.reshape(GRID_ROWS, COLS, heads, HD), (1, 0, 2, 3))

    row_out = attend_back(as_rows(query_row, H_ROW), as_rows(key_row, H_ROW), as_rows(value_row, H_ROW), as_rows(cotangent_row, H_ROW))
    col_out = attend_back(as_cols(query_col, H_COL), as_cols(key_col, H_COL), as_cols(value_col, H_COL), as_cols(cotangent_col, H_COL))
    row_flat = [piece.reshape(TOKENS, H_ROW * HD) for piece in row_out]
    col_flat = [jnp.transpose(piece, (1, 0, 2, 3)).reshape(TOKENS, H_COL * HD) for piece in col_out]
    packed = jnp.concatenate([jnp.stack(row_flat, 1), jnp.stack(col_flat, 1)], axis=-1)
    return packed.reshape(TOKENS, 3 * (H_ROW + H_COL) * HD)


def reference(query_row, key_row, value_row, cotangent_row, query_col, key_col, value_col, cotangent_col):
    grads = lax.map(section_grads, (query_row, key_row, value_row, cotangent_row, query_col, key_col, value_col, cotangent_col))
    return jnp.concatenate([grads[1:], jnp.zeros_like(grads[:1])], axis=0)
```

```python
import functools

import jax
import jax.numpy as jnp
from jax import lax
from jax.experimental import pallas as pl
from jax.experimental.pallas import tpu as pltpu
from jax.sharding import PartitionSpec as P

H_ROW = 4
H_COL = 4
HD = 128
COLS = 256


def from_behind(value, axis, steps):
    count = lax.axis_size(axis)
    leading, last = (max(0, -steps), min(count, count - steps))
    return lax.ppermute(value, axis, [(source, source + steps) for source in range(leading, last)])


def dot_nt(a, b):
    return lax.dot_general(a, b, (((1,), (1,)), ((), ())), preferred_element_type=jnp.float32)


def dot_tn(a, b):
    return lax.dot_general(a, b, (((0,), (0,)), ((), ())), preferred_element_type=jnp.float32)


def dot_nn(a, b):
    return lax.dot_general(a, b, (((1,), (0,)), ((), ())), preferred_element_type=jnp.float32)


def head_back(queries, keys, values, grad_out, allowed):
    scaling = HD ** (-0.5)
    scores = jnp.where(allowed, dot_nt(queries, keys) * scaling, -1e30)
    largest = jnp.max(scores, axis=-1, keepdims=True)
    weights = jnp.exp(scores - largest)
    probability = weights / jnp.sum(weights, axis=-1, keepdims=True)
    prob_low = probability.astype(jnp.bfloat16)
    grad_probs = dot_nt(grad_out, values)
    inner_sum = jnp.sum(prob_low.astype(jnp.float32) * grad_probs, axis=-1, keepdims=True)
    grad_low = (probability * (grad_probs - inner_sum) * scaling).astype(jnp.bfloat16)
    return (
        dot_nn(grad_low, keys).astype(jnp.bfloat16),
        dot_tn(grad_low, queries).astype(jnp.bfloat16),
        dot_tn(prob_low, grad_out).astype(jnp.bfloat16),
    )


def attend_kernel(group, q_ref, k_ref, v_ref, g_ref, dq_ref, dk_ref, dv_ref):
    tokens = q_ref.shape[0]
    query_at = lax.broadcasted_iota(jnp.int32, (tokens, tokens), 0)
    key_at = lax.broadcasted_iota(jnp.int32, (tokens, tokens), 1)
    allowed = query_at >= key_at
    if group > 1:
        allowed = allowed & ((query_at - key_at) % group == 0)
    dq, dk, dv = head_back(q_ref[...], k_ref[...], v_ref[...], g_ref[...], allowed)
    dq_ref[...] = dq
    dk_ref[...] = dk
    dv_ref[...] = dv


def attend_back(group, heads, operands, offsets):
    tokens = operands[0].shape[0]
    width = heads * HD

    def spec(offset):
        return pl.BlockSpec((tokens, HD), lambda h: (0, h + offset))

    pairs = heads * tokens * tokens
    return pl.pallas_call(
        functools.partial(attend_kernel, group),
        grid=(heads,),
        in_specs=[spec(offset) for offset in offsets],
        out_specs=[spec(0)] * 3,
        out_shape=[jax.ShapeDtypeStruct((tokens, width), jnp.bfloat16)] * 3,
        cost_estimate=pl.CostEstimate(
            flops=10 * pairs * HD, bytes_accessed=14 * tokens * width, transcendentals=pairs
        ),
    )(*operands)


def on_device(
    query_row, key_row, value_row, cotangent_row, query_col, key_col, value_col, cotangent_col
):
    tokens_dev, width = query_row.shape[1:]
    groups = lax.axis_size("seq")
    col_group = COLS // groups
    sent = jnp.concatenate([query_col[0], key_col[0], value_col[0], cotangent_col[0]], axis=-1)
    sent = sent.reshape(groups, col_group, 4 * width)
    arrived = lax.all_to_all(sent, "seq", split_axis=0, concat_axis=0, tiled=True)
    arrived = arrived.reshape(groups * col_group, 4 * width)

    row_part = attend_back(
        1, H_ROW, (query_row[0], key_row[0], value_row[0], cotangent_row[0]), (0, 0, 0, 0)
    )
    row_pack = from_behind(jnp.concatenate(row_part, axis=-1), "section", -1)

    col_part = attend_back(
        col_group, H_COL, (arrived,) * 4, (0, H_COL, 2 * H_COL, 3 * H_COL)
    )
    col_sent = jnp.concatenate(col_part, axis=-1).reshape(groups, col_group, 3 * width)
    col_pack = lax.all_to_all(col_sent, "seq", split_axis=0, concat_axis=0, tiled=True)
    col_pack = from_behind(col_pack.reshape(tokens_dev, 3 * width), "section", -1)
    pieces = []
    for i in range(3):
        pieces += [row_pack[:, i * width : (i + 1) * width], col_pack[:, i * width : (i + 1) * width]]
    return jnp.concatenate(pieces, axis=-1)[None]


def solution(mesh):
    return jax.shard_map(
        on_device,
        mesh=mesh,
        in_specs=(P("section", "seq", None),) * 8,
        out_specs=P("section", "seq", None),
        check_vma=False,
    )
```

```python
import functools

import jax
import jax.numpy as jnp
from jax import lax
from jax.experimental import pallas as pl
from jax.experimental.pallas import tpu as pltpu
from jax.sharding import PartitionSpec as P

H_ROW = 4
H_COL = 4
HD = 128
COLS = 256
LOG2E = 1.4426950408889634


def from_behind(value, axis, steps):
    count = lax.axis_size(axis)
    leading, last = (max(0, -steps), min(count, count - steps))
    return lax.ppermute(value, axis, [(source, source + steps) for source in range(leading, last)])


def dot(a, b, over_a, over_b):
    dims = (((over_a,), (over_b,)), ((), ()))
    return lax.dot_general(a, b, dims, preferred_element_type=jnp.float32)


def head_back(queries, keys, values, grad_out, allowed):
    scaling = HD ** (-0.5)
    scores = jnp.where(allowed, dot(keys, queries, 1, 1), -1e30)
    largest = jnp.max(scores, axis=0, keepdims=True)
    weights = jnp.exp2((scores - largest) * (scaling * LOG2E))
    probability = weights * (1.0 / jnp.sum(weights, axis=0, keepdims=True))
    prob_low = probability.astype(jnp.bfloat16)
    grad_probs = dot(values, grad_out, 1, 1)
    inner_sum = jnp.sum(prob_low.astype(jnp.float32) * grad_probs, axis=0, keepdims=True)
    grad_low = (probability * ((grad_probs - inner_sum) * scaling)).astype(jnp.bfloat16)
    return (
        dot(grad_low, keys, 0, 0).astype(jnp.bfloat16),
        dot(grad_low, queries, 1, 0).astype(jnp.bfloat16),
        dot(prob_low, grad_out, 1, 0).astype(jnp.bfloat16),
    )


def attend_kernel(group, heads, places, *refs):
    ins, out_ref = refs[:-1], refs[-1]
    tokens = out_ref.shape[0]
    key_at = lax.broadcasted_iota(jnp.int32, (tokens, tokens), 0)
    query_at = lax.broadcasted_iota(jnp.int32, (tokens, tokens), 1)
    allowed = query_at >= key_at
    if group > 1:
        allowed = allowed & (lax.rem(query_at, group) == lax.rem(key_at, group))
    for h in range(heads):
        taken = [ins[i][:, (at + h) * HD : (at + h + 1) * HD] for i, at in places]
        for i, grad in enumerate(head_back(*taken, allowed)):
            at = i * heads + h
            out_ref[:, at * HD : (at + 1) * HD] = grad


def attend_back(group, heads, operands, places):
    tokens = operands[0].shape[0]
    width = heads * HD
    pairs = heads * tokens * tokens
    return pl.pallas_call(
        functools.partial(attend_kernel, group, heads, places),
        in_specs=[pl.BlockSpec(memory_space=pltpu.VMEM)] * len(operands),
        out_specs=pl.BlockSpec(memory_space=pltpu.VMEM),
        out_shape=jax.ShapeDtypeStruct((tokens, 3 * width), jnp.bfloat16),
        compiler_params=pltpu.CompilerParams(vmem_limit_bytes=24 * 1024 * 1024),
        cost_estimate=pl.CostEstimate(
            flops=10 * pairs * HD, bytes_accessed=14 * tokens * width, transcendentals=pairs
        ),
    )(*operands)


def on_device(
    query_row, key_row, value_row, cotangent_row, query_col, key_col, value_col, cotangent_col
):
    tokens_dev, width = query_row.shape[1:]
    groups = lax.axis_size("seq")
    col_group = COLS // groups
    sent = jnp.concatenate([query_col[0], key_col[0], value_col[0], cotangent_col[0]], axis=-1)
    sent = sent.reshape(groups, col_group, 4 * width)
    arrived = lax.all_to_all(sent, "seq", split_axis=0, concat_axis=0, tiled=True)
    arrived = arrived.reshape(groups * col_group, 4 * width)

    row_part = attend_back(
        1,
        H_ROW,
        (query_row[0], key_row[0], value_row[0], cotangent_row[0]),
        ((0, 0), (1, 0), (2, 0), (3, 0)),
    )
    row_pack = from_behind(row_part, "section", -1)
    arrived, row_pack = lax.optimization_barrier((arrived, row_pack))

    col_part = attend_back(
        col_group, H_COL, (arrived,), ((0, 0), (0, H_COL), (0, 2 * H_COL), (0, 3 * H_COL))
    )
    col_sent = col_part.reshape(groups, col_group, 3 * width)
    col_pack = lax.all_to_all(col_sent, "seq", split_axis=0, concat_axis=0, tiled=True)
    col_pack = from_behind(col_pack.reshape(tokens_dev, 3 * width), "section", -1)
    pieces = []
    for i in range(3):
        pieces += [row_pack[:, i * width : (i + 1) * width], col_pack[:, i * width : (i + 1) * width]]
    return jnp.concatenate(pieces, axis=-1)[None]


def solution(mesh):
    return jax.shard_map(
        on_device,
        mesh=mesh,
        in_specs=(P("section", "seq", None),) * 8,
        out_specs=P("section", "seq", None),
        check_vma=False,
    )
```

```python
import functools

import jax
import jax.numpy as jnp
from jax import lax
from jax.experimental import pallas as pl
from jax.experimental.pallas import tpu as pltpu
from jax.sharding import PartitionSpec as P

H_ROW = 4
H_COL = 4
HD = 128
COLS = 256
LOG2E = 1.4426950408889634
CHUNKS = 2
AXES = ("section", "seq")
VMEM = pl.BlockSpec(memory_space=pltpu.VMEM)
SMEM = pl.BlockSpec(memory_space=pltpu.SMEM)
LEFT = pl.BlockSpec(memory_space=pl.ANY)
PARAMS = pltpu.CompilerParams(vmem_limit_bytes=24 * 1024 * 1024)


def shifted(value, steps, flip, first):
    sections, seqs = lax.axis_size("section"), lax.axis_size("seq")
    pairs = [
        (s * seqs + q, (s - steps) * seqs + (q ^ flip))
        for s in range(first, sections)
        for q in range(seqs)
    ]
    return lax.ppermute(value, AXES, pairs)


def same_half(value):
    seqs = lax.axis_size("seq")
    groups = [[q for q in range(seqs) if q % 2 == half] for half in range(2)]
    return lax.all_to_all(value, "seq", 0, 0, axis_index_groups=groups, tiled=True)


def dot(a, b, over_a, over_b):
    dims = (((over_a,), (over_b,)), ((), ()))
    return lax.dot_general(a, b, dims, preferred_element_type=jnp.float32)


def head_back(queries, keys, values, grad_out, allowed):
    scaling = HD ** (-0.5)
    scores = jnp.where(allowed, dot(keys, queries, 1, 1), -1e30)
    largest = jnp.max(scores, axis=0, keepdims=True)
    weights = jnp.exp2((scores - largest) * (scaling * LOG2E))
    probability = weights * (1.0 / jnp.sum(weights, axis=0, keepdims=True))
    prob_low = probability.astype(jnp.bfloat16)
    grad_probs = dot(values, grad_out, 1, 1)
    inner_sum = jnp.sum(prob_low.astype(jnp.float32) * grad_probs, axis=0, keepdims=True)
    grad_low = (probability * ((grad_probs - inner_sum) * scaling)).astype(jnp.bfloat16)
    return (
        dot(grad_low, keys, 0, 0).astype(jnp.bfloat16),
        dot(grad_low, queries, 1, 0).astype(jnp.bfloat16),
        dot(prob_low, grad_out, 1, 0).astype(jnp.bfloat16),
    )


def cost(heads, tokens):
    pairs = heads * tokens * tokens
    return pl.CostEstimate(
        flops=10 * pairs * HD, bytes_accessed=14 * tokens * heads * HD, transcendentals=pairs
    )


def row_kernel(q_ref, k_ref, v_ref, g_ref, out_ref):
    tokens = out_ref.shape[0]
    key_at = lax.broadcasted_iota(jnp.int32, (tokens, tokens), 0)
    query_at = lax.broadcasted_iota(jnp.int32, (tokens, tokens), 1)
    allowed = query_at >= key_at
    for h in range(H_ROW):
        lanes = slice(h * HD, (h + 1) * HD)
        taken = [ref[:, lanes] for ref in (q_ref, k_ref, v_ref, g_ref)]
        for i, grad in enumerate(head_back(*taken, allowed)):
            at = i * H_ROW + h
            out_ref[:, at * HD : (at + 1) * HD] = grad


def row_grads(operands):
    tokens = operands[0].shape[0]
    return pl.pallas_call(
        row_kernel,
        in_specs=[VMEM] * 4,
        out_specs=VMEM,
        out_shape=jax.ShapeDtypeStruct((tokens, 3 * H_ROW * HD), jnp.bfloat16),
        compiler_params=PARAMS,
        cost_estimate=cost(H_ROW, tokens),
    )(*operands)


def pack_kernel(start, half_ref, q_ref, k_ref, v_ref, g_ref, *refs):
    out_ref = refs[-1]
    group = out_ref.shape[1] // 2
    width = out_ref.shape[2] // 4
    for i, ref in enumerate((q_ref, k_ref, v_ref, g_ref)):
        for part in range(2):
            first = pl.multiple_of((half_ref[0] ^ part) * group, group)
            out_ref[:, part * group : (part + 1) * group, i * width : (i + 1) * width] = ref[
                :, pl.ds(first, group), start : start + width
            ]


def pack(half, operands, chunk, after):
    rows, columns, lanes = operands[0].shape
    width = lanes // CHUNKS
    return pl.pallas_call(
        functools.partial(pack_kernel, chunk * width),
        in_specs=[SMEM] + [VMEM] * 4 + [LEFT] * len(after),
        out_specs=VMEM,
        out_shape=jax.ShapeDtypeStruct((rows, columns, 4 * width), jnp.bfloat16),
        compiler_params=PARAMS,
        cost_estimate=pl.CostEstimate(
            flops=0, bytes_accessed=4 * rows * columns * 4 * width, transcendentals=0
        ),
    )(half, *operands, *after)


def col_kernel(half_ref, own_ref, far_ref, *refs):
    own_out, far_out = refs[-2:]
    rows, group, lanes = far_ref.shape
    width = lanes // 4
    heads = width // HD
    tokens = rows * group

    def place(dim):
        at = lax.broadcasted_iota(jnp.int32, (2 * tokens, 2 * tokens), dim)
        far = (at >= tokens).astype(jnp.int32)
        grid_row = 2 * ((at - far * tokens) // group) + (half_ref[0] ^ far)
        return grid_row, lax.rem(at, group)

    key_row, key_col = place(0)
    query_row, query_col = place(1)
    allowed = (query_row >= key_row) & (query_col == key_col)
    for h in range(heads):
        taken = []
        for i in range(4):
            lane = slice(i * width + h * HD, i * width + (h + 1) * HD)
            taken.append(
                jnp.concatenate(
                    [
                        own_ref[:, :group, lane].reshape(tokens, HD),
                        far_ref[:, :, lane].reshape(tokens, HD),
                    ],
                    axis=0,
                )
            )
        for i, grad in enumerate(head_back(*taken, allowed)):
            lane = slice(i * width + h * HD, i * width + (h + 1) * HD)
            own_out[:, :, lane] = grad[:tokens].reshape(rows, group, HD)
            far_out[:, :, lane] = grad[tokens:].reshape(rows, group, HD)


def col_grads(half, own, far, after):
    rows, group, lanes = far.shape
    result = jax.ShapeDtypeStruct((rows, group, 3 * lanes // 4), jnp.bfloat16)
    return pl.pallas_call(
        col_kernel,
        in_specs=[SMEM, VMEM, VMEM] + [LEFT] * len(after),
        out_specs=[VMEM, VMEM],
        out_shape=[result, result],
        compiler_params=PARAMS,
        cost_estimate=cost(lanes // 4 // HD, 2 * rows * group),
    )(half, own, far, *after)


def join_kernel(own_ref, far_ref, *refs):
    group = own_ref.shape[1]
    refs[-1][:, :group, :] = own_ref[...]
    refs[-1][:, group:, :] = far_ref[...]


def join(own, far, after):
    rows, group, lanes = own.shape
    return pl.pallas_call(
        join_kernel,
        in_specs=[VMEM, VMEM] + [LEFT] * len(after),
        out_specs=VMEM,
        out_shape=jax.ShapeDtypeStruct((rows, 2 * group, lanes), jnp.bfloat16),
        compiler_params=PARAMS,
        cost_estimate=pl.CostEstimate(
            flops=0, bytes_accessed=8 * rows * group * lanes, transcendentals=0
        ),
    )(own, far, *after)


def unpack_kernel(half_ref, row_ref, *refs):
    parts, out_ref = refs[:-1], refs[-1]
    group = out_ref.shape[1] // 2
    wide = out_ref.shape[2] // 6
    width = wide // CHUNKS
    for i in range(3):
        out_ref[:, :, 2 * i * wide : (2 * i + 1) * wide] = row_ref[:, :, i * wide : (i + 1) * wide]
        for c, ref in enumerate(parts):
            lane = (2 * i + 1) * wide + c * width
            for part in range(2):
                first = pl.multiple_of((half_ref[0] ^ part) * group, group)
                out_ref[:, part * group : (part + 1) * group, lane : lane + width] = ref[
                    :, pl.ds(first, group), i * width : (i + 1) * width
                ]


def unpack(half, row_part, parts):
    rows, columns, lanes = row_part.shape
    return pl.pallas_call(
        unpack_kernel,
        in_specs=[SMEM] + [VMEM] * (1 + len(parts)),
        out_specs=VMEM,
        out_shape=jax.ShapeDtypeStruct((rows, columns, 2 * lanes), jnp.bfloat16),
        compiler_params=PARAMS,
        cost_estimate=pl.CostEstimate(
            flops=0, bytes_accessed=8 * rows * columns * lanes, transcendentals=0
        ),
    )(half, row_part, *parts)


def on_device(
    query_row, key_row, value_row, cotangent_row, query_col, key_col, value_col, cotangent_col
):
    tokens_dev, width = query_row.shape[1:]
    places = lax.axis_size("seq") // 2
    columns = COLS // places
    group = columns // 2
    half = lax.rem(lax.axis_index("seq"), 2).astype(jnp.int32).reshape(1)
    col_in = [
        block[0].reshape(places, columns, width)
        for block in (query_col, key_col, value_col, cotangent_col)
    ]

    row_part = row_grads((query_row[0], key_row[0], value_row[0], cotangent_row[0]))
    near = [same_half(pack(half, col_in, 0, ()))]
    sent = [near[0][:, group:]]
    far = [shifted(sent[0], 0, 1, 1)]
    row_pack = shifted(row_part, 1, 0, 1)
    near.append(same_half(pack(half, col_in, 1, (row_part,))))
    sent.append(near[1][:, group:])
    far.append(shifted(sent[1], 0, 1, 1))
    own, distant = col_grads(half, near[0], far[0], (sent[1],))
    back = [(shifted(distant, 1, 1, 1), shifted(own, 1, 0, 1))]
    own, distant = col_grads(half, near[1], far[1], ())
    back.append((shifted(distant, 1, 1, 1), shifted(own, 1, 0, 1)))
    parts = [same_half(join(back[0][1], back[0][0], (own,)))]
    parts.append(same_half(join(back[1][1], back[1][0], ())))
    result = unpack(half, row_pack.reshape(places, columns, 3 * width), parts)
    return result.reshape(1, tokens_dev, 6 * width)


def solution(mesh):
    return jax.shard_map(
        on_device,
        mesh=mesh,
        in_specs=(P("section", "seq", None),) * 8,
        out_specs=P("section", "seq", None),
        check_vma=False,
    )
```

```python
import functools

import jax
import jax.numpy as jnp
from jax import lax
from jax.experimental import pallas as pl
from jax.experimental.pallas import tpu as pltpu
from jax.sharding import PartitionSpec as P

H_ROW = 4
H_COL = 4
HD = 128
COLS = 256
LOG2E = 1.4426950408889634
VMEM = pl.BlockSpec(memory_space=pltpu.VMEM)
LEFT = pl.BlockSpec(memory_space=pl.ANY)
PARAMS = pltpu.CompilerParams(vmem_limit_bytes=24 * 1024 * 1024)


def from_behind(value, axis, steps):
    count = lax.axis_size(axis)
    leading, last = (max(0, -steps), min(count, count - steps))
    return lax.ppermute(value, axis, [(source, source + steps) for source in range(leading, last)])


def dot(a, b, over_a, over_b):
    dims = (((over_a,), (over_b,)), ((), ()))
    return lax.dot_general(a, b, dims, preferred_element_type=jnp.float32)


def head_back(queries, keys, values, grad_out, allowed):
    scaling = HD ** (-0.5)
    scores = jnp.where(allowed, dot(keys, queries, 1, 1), -1e30)
    largest = jnp.max(scores, axis=0, keepdims=True)
    weights = jnp.exp2((scores - largest) * (scaling * LOG2E))
    probability = weights * (1.0 / jnp.sum(weights, axis=0, keepdims=True))
    prob_low = probability.astype(jnp.bfloat16)
    grad_probs = dot(values, grad_out, 1, 1)
    inner_sum = jnp.sum(prob_low.astype(jnp.float32) * grad_probs, axis=0, keepdims=True)
    grad_low = (probability * ((grad_probs - inner_sum) * scaling)).astype(jnp.bfloat16)
    return (
        dot(grad_low, keys, 0, 0).astype(jnp.bfloat16),
        dot(grad_low, queries, 1, 0).astype(jnp.bfloat16),
        dot(prob_low, grad_out, 1, 0).astype(jnp.bfloat16),
    )


def cost(heads, tokens):
    pairs = heads * tokens * tokens
    return pl.CostEstimate(
        flops=10 * pairs * HD, bytes_accessed=14 * tokens * heads * HD, transcendentals=pairs
    )


def moved(nbytes):
    return pl.CostEstimate(flops=0, bytes_accessed=2 * nbytes, transcendentals=0)


def row_kernel(q_hbm, k_hbm, v_hbm, g_hbm, out_ref, held, sems):
    tokens = out_ref.shape[0]
    copies = [
        pltpu.make_async_copy(ref, held.at[i], sems.at[i])
        for i, ref in enumerate((q_hbm, k_hbm, v_hbm, g_hbm))
    ]
    for copy in copies:
        copy.start()
    key_at = lax.broadcasted_iota(jnp.int32, (tokens, tokens), 0)
    query_at = lax.broadcasted_iota(jnp.int32, (tokens, tokens), 1)
    allowed = query_at >= key_at
    for copy in copies:
        copy.wait()
    for h in range(H_ROW):
        taken = [held[i, :, h * HD : (h + 1) * HD] for i in range(4)]
        for i, grad in enumerate(head_back(*taken, allowed)):
            at = i * H_ROW + h
            out_ref[:, at * HD : (at + 1) * HD] = grad


def row_grads(*operands):
    tokens, width = operands[0].shape
    return pl.pallas_call(
        row_kernel,
        in_specs=[LEFT] * 4,
        out_specs=VMEM,
        out_shape=jax.ShapeDtypeStruct((tokens, 3 * width), jnp.bfloat16),
        scratch_shapes=[
            pltpu.VMEM((4, tokens, width), jnp.bfloat16),
            pltpu.SemaphoreType.DMA((4,)),
        ],
        compiler_params=PARAMS,
        cost_estimate=cost(H_ROW, tokens),
    )(*operands)


def col_kernel(group, in_ref, out_ref):
    tokens = out_ref.shape[0]
    key_at = lax.broadcasted_iota(jnp.int32, (tokens, tokens), 0)
    query_at = lax.broadcasted_iota(jnp.int32, (tokens, tokens), 1)
    same = lax.rem(query_at, group) == lax.rem(key_at, group)
    allowed = (query_at >= key_at) & same
    for h in range(H_COL):
        lanes = [slice((i * H_COL + h) * HD, (i * H_COL + h + 1) * HD) for i in range(4)]
        taken = [in_ref[:, lane] for lane in lanes]
        for lane, grad in zip(lanes, head_back(*taken, allowed)):
            out_ref[:, lane] = grad


def col_grads(group, operand):
    tokens, lanes = operand.shape
    return pl.pallas_call(
        functools.partial(col_kernel, group),
        in_specs=[VMEM],
        out_specs=VMEM,
        out_shape=jax.ShapeDtypeStruct((tokens, 3 * lanes // 4), jnp.bfloat16),
        compiler_params=PARAMS,
        cost_estimate=cost(H_COL, tokens),
    )(operand)


def keep_kernel(in_ref, after_ref, out_ref):
    out_ref[...] = in_ref[...]


def keep(value, after):
    return pl.pallas_call(
        keep_kernel,
        in_specs=[VMEM, LEFT],
        out_specs=VMEM,
        out_shape=jax.ShapeDtypeStruct(value.shape, value.dtype),
        compiler_params=PARAMS,
        cost_estimate=moved(2 * value.size),
    )(value, after)


def place_kernel(row_ref, col_ref, out_ref):
    width = row_ref.shape[1] // 3
    for i in range(3):
        lanes = slice(i * width, (i + 1) * width)
        out_ref[:, 2 * i * width : (2 * i + 1) * width] = row_ref[:, lanes]
        out_ref[:, (2 * i + 1) * width : (2 * i + 2) * width] = col_ref[:, lanes]


def place(row_part, col_part):
    tokens, lanes = row_part.shape
    return pl.pallas_call(
        place_kernel,
        in_specs=[VMEM] * 2,
        out_specs=VMEM,
        out_shape=jax.ShapeDtypeStruct((tokens, 2 * lanes), jnp.bfloat16),
        compiler_params=PARAMS,
        cost_estimate=moved(4 * tokens * lanes),
    )(row_part, col_part)


def exchanged(value):
    return lax.all_to_all(value, "seq", split_axis=0, concat_axis=0, tiled=True)


def col_path(query_col, key_col, value_col, cotangent_col):
    tokens_dev, width = query_col.shape
    groups = lax.axis_size("seq")
    group = COLS // groups
    sent = jnp.concatenate([query_col, key_col, value_col, cotangent_col], axis=-1)
    arrived = exchanged(sent.reshape(groups, group, 4 * width))
    grads = col_grads(group, arrived.reshape(groups * group, 4 * width))
    back = exchanged(grads.reshape(groups, group, 3 * width))
    return back.reshape(tokens_dev, 3 * width)


def no_col_path(query_col, key_col, value_col, cotangent_col):
    tokens_dev, width = query_col.shape
    return jnp.zeros((tokens_dev, 3 * width), query_col.dtype)


def on_device(
    query_row, key_row, value_row, cotangent_row, query_col, key_col, value_col, cotangent_col
):
    row_part = row_grads(query_row[0], key_row[0], value_row[0], cotangent_row[0])
    row_pack = from_behind(row_part, "section", -1)
    col_part = lax.cond(
        lax.axis_index("section") > 0,
        col_path,
        no_col_path,
        query_col[0],
        key_col[0],
        value_col[0],
        cotangent_col[0],
    )
    col_pack = from_behind(keep(col_part, row_pack), "section", -1)
    return place(row_pack, col_pack)[None]


def solution(mesh):
    return jax.shard_map(
        on_device,
        mesh=mesh,
        in_specs=(P("section", "seq", None),) * 8,
        out_specs=P("section", "seq", None),
        check_vma=False,
    )
```

```python
import functools

import jax
import jax.numpy as jnp
from jax import lax
from jax.experimental import pallas as pl
from jax.experimental.pallas import tpu as pltpu
from jax.sharding import PartitionSpec as P

H_ROW = 4
H_COL = 4
HD = 128
COLS = 256
LOG2E = 1.4426950408889634
VMEM = pl.BlockSpec(memory_space=pltpu.VMEM)
LEFT = pl.BlockSpec(memory_space=pl.ANY)
PARAMS = pltpu.CompilerParams(vmem_limit_bytes=24 * 1024 * 1024)


def from_behind(value, axis, steps):
    count = lax.axis_size(axis)
    leading, last = (max(0, -steps), min(count, count - steps))
    return lax.ppermute(value, axis, [(source, source + steps) for source in range(leading, last)])


def dot(a, b, over_a, over_b):
    dims = (((over_a,), (over_b,)), ((), ()))
    return lax.dot_general(a, b, dims, preferred_element_type=jnp.float32)


def head_back(queries, keys, values, grad_out, allowed):
    scaling = HD ** (-0.5)
    scores = jnp.where(allowed, dot(keys, queries, 1, 1), -1e30)
    largest = jnp.max(scores, axis=0, keepdims=True)
    weights = jnp.exp2((scores - largest) * (scaling * LOG2E))
    probability = weights * (1.0 / jnp.sum(weights, axis=0, keepdims=True))
    prob_low = probability.astype(jnp.bfloat16)
    grad_probs = dot(values, grad_out, 1, 1)
    inner_sum = jnp.sum(prob_low.astype(jnp.float32) * grad_probs, axis=0, keepdims=True)
    grad_low = (probability * ((grad_probs - inner_sum) * scaling)).astype(jnp.bfloat16)
    return (
        dot(grad_low, keys, 0, 0).astype(jnp.bfloat16),
        dot(grad_low, queries, 1, 0).astype(jnp.bfloat16),
        dot(prob_low, grad_out, 1, 0).astype(jnp.bfloat16),
    )


def cost(heads, tokens):
    pairs = heads * tokens * tokens
    return pl.CostEstimate(
        flops=10 * pairs * HD, bytes_accessed=14 * tokens * heads * HD, transcendentals=pairs
    )


def moved(nbytes):
    return pl.CostEstimate(flops=0, bytes_accessed=2 * nbytes, transcendentals=0)


def row_kernel(q_hbm, k_hbm, v_hbm, g_hbm, out_ref, held, sems):
    tokens = out_ref.shape[0]
    copies = [
        pltpu.make_async_copy(ref, held.at[i], sems.at[i])
        for i, ref in enumerate((q_hbm, k_hbm, v_hbm, g_hbm))
    ]
    for copy in copies:
        copy.start()
    key_at = lax.broadcasted_iota(jnp.int32, (tokens, tokens), 0)
    query_at = lax.broadcasted_iota(jnp.int32, (tokens, tokens), 1)
    allowed = query_at >= key_at
    for copy in copies:
        copy.wait()
    for h in range(H_ROW):
        taken = [held[i, :, h * HD : (h + 1) * HD] for i in range(4)]
        for i, grad in enumerate(head_back(*taken, allowed)):
            at = i * H_ROW + h
            out_ref[:, at * HD : (at + 1) * HD] = grad


def row_grads(*operands):
    tokens, width = operands[0].shape
    return pl.pallas_call(
        row_kernel,
        in_specs=[LEFT] * 4,
        out_specs=VMEM,
        out_shape=jax.ShapeDtypeStruct((tokens, 3 * width), jnp.bfloat16),
        scratch_shapes=[
            pltpu.VMEM((4, tokens, width), jnp.bfloat16),
            pltpu.SemaphoreType.DMA((4,)),
        ],
        cost_estimate=cost(H_ROW, tokens),
    )(*operands)


def col_kernel(group, *refs):
    ins, out_ref = refs[:-1], refs[-1]
    tokens = out_ref.shape[0]
    key_at = lax.broadcasted_iota(jnp.int32, (tokens, tokens), 0)
    query_at = lax.broadcasted_iota(jnp.int32, (tokens, tokens), 1)
    same = lax.rem(query_at, group) == lax.rem(key_at, group)
    allowed = (query_at >= key_at) & same
    done = 0
    for ref in ins:
        held = ref.shape[1] // (4 * HD)
        for h in range(held):
            lanes = [slice((i * held + h) * HD, (i * held + h + 1) * HD) for i in range(4)]
            taken = [ref[:, lane] for lane in lanes]
            for i, grad in enumerate(head_back(*taken, allowed)):
                at = i * H_COL + done + h
                out_ref[:, at * HD : (at + 1) * HD] = grad
        done += held


def col_grads(group, operands):
    tokens = operands[0].shape[0]
    return pl.pallas_call(
        functools.partial(col_kernel, group),
        in_specs=[VMEM] * len(operands),
        out_specs=VMEM,
        out_shape=jax.ShapeDtypeStruct((tokens, 3 * H_COL * HD), jnp.bfloat16),
        compiler_params=PARAMS,
        cost_estimate=cost(H_COL, tokens),
    )(*operands)


def place_kernel(row_ref, col_ref, out_ref):
    width = row_ref.shape[1] // 3
    for i in range(3):
        lanes = slice(i * width, (i + 1) * width)
        out_ref[:, 2 * i * width : (2 * i + 1) * width] = row_ref[:, lanes]
        out_ref[:, (2 * i + 1) * width : (2 * i + 2) * width] = col_ref[:, lanes]


def place(row_part, col_part):
    tokens, lanes = row_part.shape
    return pl.pallas_call(
        place_kernel,
        in_specs=[VMEM] * 2,
        out_specs=VMEM,
        out_shape=jax.ShapeDtypeStruct((tokens, 2 * lanes), jnp.bfloat16),
        compiler_params=PARAMS,
        cost_estimate=moved(4 * tokens * lanes),
    )(row_part, col_part)


def exchanged(value):
    return lax.all_to_all(value, "seq", split_axis=0, concat_axis=0, tiled=True)


def col_path(parts, block):
    tokens_dev, lanes = block.shape
    width = lanes // 4
    groups = lax.axis_size("seq")
    group = COLS // groups
    arrived, done = [], 0
    for heads in parts:
        step = heads * HD
        sent = block
        if step < width:
            first = [i * width + done for i in range(4)]
            sent = jnp.concatenate([block[:, at : at + step] for at in first], axis=-1)
        sent = exchanged(sent.reshape(groups, group, 4 * step))
        arrived.append(sent.reshape(groups * group, 4 * step))
        done += step
    back = exchanged(col_grads(group, arrived).reshape(groups, group, 3 * width))
    return back.reshape(tokens_dev, 3 * width)


def no_col_path(block):
    tokens_dev, lanes = block.shape
    return jnp.zeros((tokens_dev, 3 * lanes // 4), block.dtype)


def on_device(
    query_row, key_row, value_row, cotangent_row, query_col, key_col, value_col, cotangent_col
):
    col_in = jnp.concatenate([query_col[0], key_col[0], value_col[0], cotangent_col[0]], axis=-1)
    col_in = from_behind(col_in, "section", -1)
    row_part = row_grads(query_row[0], key_row[0], value_row[0], cotangent_row[0])
    row_pack = from_behind(row_part, "section", -1)
    section = lax.axis_index("section")
    place_z = section // 2
    branch = jnp.where(section == lax.axis_size("section") - 1, 0, jnp.where(place_z == 5, 2, 1))
    col_part = lax.switch(
        branch,
        [
            no_col_path,
            functools.partial(col_path, (4,)),
            functools.partial(col_path, (1, 3)),
        ],
        col_in,
    )
    return place(row_pack, col_part)[None]


def solution(mesh):
    return jax.shard_map(
        on_device,
        mesh=mesh,
        in_specs=(P("section", "seq", None),) * 8,
        out_specs=P("section", "seq", None),
        check_vma=False,
    )
```

```python
import functools

import jax
import jax.numpy as jnp
from jax import lax
from jax.experimental import pallas as pl
from jax.experimental.pallas import tpu as pltpu
from jax.sharding import PartitionSpec as P

H_ROW = 4
H_COL = 4
HD = 128
COLS = 256
LOG2E = 1.4426950408889634
VMEM = pl.BlockSpec(memory_space=pltpu.VMEM)
LEFT = pl.BlockSpec(memory_space=pl.ANY)
PARAMS = pltpu.CompilerParams(vmem_limit_bytes=24 * 1024 * 1024)


def from_behind(value, axis, steps):
    count = lax.axis_size(axis)
    leading, last = (max(0, -steps), min(count, count - steps))
    return lax.ppermute(value, axis, [(source, source + steps) for source in range(leading, last)])


def dot(a, b, over_a, over_b):
    dims = (((over_a,), (over_b,)), ((), ()))
    return lax.dot_general(a, b, dims, preferred_element_type=jnp.float32)


def head_back(queries, keys, values, grad_out, allowed):
    scaling = HD ** (-0.5)
    scores = jnp.where(allowed, dot(keys, queries, 1, 1), -1e30)
    largest = jnp.max(scores, axis=0, keepdims=True)
    weights = jnp.exp2((scores - largest) * (scaling * LOG2E))
    probability = weights * (1.0 / jnp.sum(weights, axis=0, keepdims=True))
    prob_low = probability.astype(jnp.bfloat16)
    grad_probs = dot(values, grad_out, 1, 1)
    inner_sum = jnp.sum(prob_low.astype(jnp.float32) * grad_probs, axis=0, keepdims=True)
    grad_low = (probability * ((grad_probs - inner_sum) * scaling)).astype(jnp.bfloat16)
    return (
        dot(grad_low, keys, 0, 0),
        dot(grad_low, queries, 1, 0),
        dot(prob_low, grad_out, 1, 0),
    )


def causal_back(queries, keys, values, grad_out, allowed):
    half = queries.shape[0] // 2
    early, late = slice(0, half), slice(half, 2 * half)
    first = head_back(
        queries[early], keys[early], values[early], grad_out[early], allowed[early, early]
    )
    second = head_back(queries[late], keys, values, grad_out[late], allowed[:, late])
    pairs = [(first[0], second[0])]
    pairs += [(a + b[early], b[late]) for a, b in zip(first[1:], second[1:])]
    return [jnp.concatenate(pair, axis=0).astype(jnp.bfloat16) for pair in pairs]


def cost(heads, tokens):
    pairs = heads * tokens * tokens
    return pl.CostEstimate(
        flops=10 * pairs * HD, bytes_accessed=14 * tokens * heads * HD, transcendentals=pairs
    )


def moved(nbytes):
    return pl.CostEstimate(flops=0, bytes_accessed=2 * nbytes, transcendentals=0)


def row_kernel(q_hbm, k_hbm, v_hbm, g_hbm, out_ref, held, sems):
    tokens = out_ref.shape[0]
    copies = [
        pltpu.make_async_copy(ref, held.at[i], sems.at[i])
        for i, ref in enumerate((q_hbm, k_hbm, v_hbm, g_hbm))
    ]
    for copy in copies:
        copy.start()
    key_at = lax.broadcasted_iota(jnp.int32, (tokens, tokens), 0)
    query_at = lax.broadcasted_iota(jnp.int32, (tokens, tokens), 1)
    allowed = query_at >= key_at
    for copy in copies:
        copy.wait()
    for h in range(H_ROW):
        taken = [held[i, :, h * HD : (h + 1) * HD] for i in range(4)]
        for i, grad in enumerate(causal_back(*taken, allowed)):
            at = i * H_ROW + h
            out_ref[:, at * HD : (at + 1) * HD] = grad


def row_grads(*operands):
    tokens, width = operands[0].shape
    return pl.pallas_call(
        row_kernel,
        in_specs=[LEFT] * 4,
        out_specs=VMEM,
        out_shape=jax.ShapeDtypeStruct((tokens, 3 * width), jnp.bfloat16),
        scratch_shapes=[
            pltpu.VMEM((4, tokens, width), jnp.bfloat16),
            pltpu.SemaphoreType.DMA((4,)),
        ],
        cost_estimate=cost(H_ROW, tokens),
    )(*operands)


def col_kernel(group, *refs):
    ins, out_ref = refs[:-1], refs[-1]
    tokens = out_ref.shape[0]
    key_at = lax.broadcasted_iota(jnp.int32, (tokens, tokens), 0)
    query_at = lax.broadcasted_iota(jnp.int32, (tokens, tokens), 1)
    same = lax.rem(query_at, group) == lax.rem(key_at, group)
    allowed = (query_at >= key_at) & same
    places = [
        (ref, slice(at, at + HD)) for ref in ins for at in range(0, ref.shape[1], HD)
    ]
    for h in range(H_COL):
        taken = [ref[:, lane] for ref, lane in places[h::H_COL]]
        for i, grad in enumerate(causal_back(*taken, allowed)):
            at = i * H_COL + h
            out_ref[:, at * HD : (at + 1) * HD] = grad


def col_grads(group, operands):
    tokens = operands[0].shape[0]
    return pl.pallas_call(
        functools.partial(col_kernel, group),
        in_specs=[VMEM] * len(operands),
        out_specs=VMEM,
        out_shape=jax.ShapeDtypeStruct((tokens, 3 * H_COL * HD), jnp.bfloat16),
        compiler_params=PARAMS,
        cost_estimate=cost(H_COL, tokens),
    )(*operands)


def place_kernel(row_ref, col_ref, out_ref):
    width = row_ref.shape[1] // 3
    for i in range(3):
        lanes = slice(i * width, (i + 1) * width)
        out_ref[:, 2 * i * width : (2 * i + 1) * width] = row_ref[:, lanes]
        out_ref[:, (2 * i + 1) * width : (2 * i + 2) * width] = col_ref[:, lanes]


def place(row_part, col_part):
    tokens, lanes = row_part.shape
    return pl.pallas_call(
        place_kernel,
        in_specs=[VMEM] * 2,
        out_specs=VMEM,
        out_shape=jax.ShapeDtypeStruct((tokens, 2 * lanes), jnp.bfloat16),
        compiler_params=PARAMS,
        cost_estimate=moved(4 * tokens * lanes),
    )(row_part, col_part)


def exchanged(value):
    return lax.all_to_all(value, "seq", split_axis=0, concat_axis=0, tiled=True)


def col_path(first, block):
    tokens_dev, lanes = block.shape
    groups = lax.axis_size("seq")
    group = COLS // groups
    arrived = []
    for part in (block[:, :first], block[:, first:]) if first else (block,):
        width = part.shape[1]
        sent = exchanged(part.reshape(groups, group, width))
        arrived.append(sent.reshape(groups * group, width))
    grads = col_grads(group, arrived)
    back = exchanged(grads.reshape(groups, group, grads.shape[1]))
    return back.reshape(tokens_dev, grads.shape[1])


def no_col_path(block):
    tokens_dev, lanes = block.shape
    return jnp.zeros((tokens_dev, 3 * lanes // 4), block.dtype)


def on_device(
    query_row, key_row, value_row, cotangent_row, query_col, key_col, value_col, cotangent_col
):
    col_in = jnp.concatenate([query_col[0], key_col[0], value_col[0], cotangent_col[0]], axis=-1)
    col_in = from_behind(col_in, "section", -1)
    row_part = row_grads(query_row[0], key_row[0], value_row[0], cotangent_row[0])
    row_pack = from_behind(row_part, "section", -1)
    section = lax.axis_index("section")
    place_z = section // 2
    behaviour = jnp.where(place_z == 5, 2, 1)
    branch = jnp.where(section == lax.axis_size("section") - 1, 0, behaviour)
    col_part = lax.switch(
        branch,
        [
            no_col_path,
            functools.partial(col_path, 0),
            functools.partial(col_path, 512),
        ],
        col_in,
    )
    return place(row_pack, col_part)[None]


def solution(mesh):
    return jax.shard_map(
        on_device,
        mesh=mesh,
        in_specs=(P("section", "seq", None),) * 8,
        out_specs=P("section", "seq", None),
        check_vma=False,
    )
```
